32 devices in a mesh: shot: 4 (over z), pair: 2 (over y), space: 4 (over x, core).
Axes of the slice: x: 2, y: 2, z: 4, core: 2. Of those that a mesh axis runs over, the one named last changes fastest.
Arguments:
- states: float32 [4, 2, 2, 64, 128, 128], P('shot', 'pair', None, 'space'), may hold values from -4 to 4
- courant: float32 [64, 128, 128], P('space'), may hold values from 0.05 to 0.2
- records: float32 [4, 12, 64, 128], P('shot', None, 'space'), may hold values from -6 to 6
Outputs:
- imaging: float32 [64, 128, 128], P('space', 'shot', 'pair')
The draws below stay inside these ranges and needn't reach their ends.
All inputs are finite; a program needn't handle non-finite values.
Results may differ from the reference program's by a relative error of at most 0.00002.
Values sent between devices are 32-bit elements; how exact they have to be, the bound alone decides.
No kernel may reach another device: no remote copies, remote signals or barrier semaphores. Data moves between devices by JAX's collectives and lax.ppermute only.
A program may use at most 64 MiB of HBM per device.

```python
import math
import jax
import jax.numpy as jnp
from jax import lax

NY = 128
NZ = 128
STEPS = 12
IMAGE_EVERY = 2
NX = 64
SHOTS = 4


def block_scale(stream_key, shape, pieces, smallest, largest):
    level, own = 1.0, jax.random.fold_in(stream_key, 6)
    for position, blocks in pieces:
        draws = jnp.exp(jax.random.uniform(jax.random.fold_in(own, position), (blocks,), jnp.float32, smallest / len(pieces), largest / len(pieces)))
        level = level * jnp.repeat(draws, shape[position] // blocks).reshape([-1 if axis == position else 1 for axis in range(len(shape))])
    return level


def centred(own_key, dims, deviation, limit, shards=(), kind=jnp.bfloat16):
    entries = deviation * jax.random.normal(own_key, dims, jnp.float32)
    if shards:
        entries = entries * block_scale(own_key, dims, shards, -0.22, 0.18)
    return jnp.clip(entries, -limit, limit).astype(kind)


def setup_inputs(seed: int = 0) -> dict:
    keys = jax.random.split(jax.random.key(seed), 4)
    states = centred(keys[0], (SHOTS, 2, 2, NX, NY, NZ), 0.5, 4.0, ((0, 4), (1, 2), (3, 4)), jnp.float32)
    courant = jnp.clip(jnp.exp(math.log(0.2) - 1.3862944 * jax.random.uniform(keys[1], (NX, NY, NZ), jnp.float32) ** block_scale(keys[1], (NX, NY, NZ), ((0, 4),), -0.2, 0.2)), 0.05, 0.2)
    records = centred(keys[2], (SHOTS, STEPS, NX, NY), 1.0, 6.0, ((0, 4), (2, 4)), jnp.float32)
    return {"states": states, "courant": courant, "records": records}


def laplacian(extended, center):
    base = center.ndim - 3

    def along(whole, dim_axis, extent):
        def shifted(start):
            return lax.slice_in_dim(whole, start, start + extent, axis=dim_axis)
        return (-shifted(0) + 16.0 * shifted(1) - 30.0 * shifted(2) + 16.0 * shifted(3) - shifted(4)) / 12.0

    widths_y = [(0, 0)] * base + [(0, 0), (2, 2), (0, 0)]
    widths_z = [(0, 0)] * base + [(0, 0), (0, 0), (2, 2)]
    total = along(extended, base, center.shape[base])
    total = total + along(jnp.pad(center, widths_y), base + 1, center.shape[base + 1])
    total = total + along(jnp.pad(center, widths_z), base + 2, center.shape[base + 2])
    return total


def advance(earlier, current, courant):
    extended = jnp.pad(current, ((2, 2), (0, 0), (0, 0)))
    return 2.0 * current - earlier + courant * laplacian(extended, current)


def reference(states, courant, records):
    total_image = jnp.zeros(courant.shape, jnp.float32)
    weight = IMAGE_EVERY / STEPS
    for shot_index in range(SHOTS):
        source_old = states[shot_index, 0, 0]
        source_now = states[shot_index, 0, 1]
        receiver_old = states[shot_index, 1, 0]
        receiver_now = states[shot_index, 1, 1]
        shot_image = jnp.zeros(courant.shape, jnp.float32)
        for tick_index in range(STEPS):
            advanced = advance(source_old, source_now, courant)
            source_old, source_now = source_now, advanced
            advanced = advance(receiver_old, receiver_now, courant)
            advanced = advanced.at[:, :, 0].add(records[shot_index, tick_index])
            receiver_old, receiver_now = receiver_now, advanced
            if (tick_index + 1) % IMAGE_EVERY == 0:
                shot_image = shot_image + source_now * receiver_now
        total_image = total_image + shot_image * weight
    return total_image
```

```python
import functools

import jax
import jax.numpy as jnp
from jax import lax
from jax.experimental import pallas as pl
from jax.experimental.pallas import tpu as pltpu
from jax.sharding import PartitionSpec as P

STEPS = 12
IMAGE_EVERY = 2
GROUP = 4
F32 = jnp.float32
VM = pl.BlockSpec(memory_space=pltpu.VMEM)
SM = pl.BlockSpec(memory_space=pltpu.SMEM)
LIMIT = 56 << 20
HC = 6
DEPTH = 8
TPAD = 16


def sds(*shape):
    return jax.ShapeDtypeStruct(shape, F32)


def call(kernel, outs, scratch, *args, flops=1, name=None):
    moved = sum(4 * a.size for a in args) + sum(4 * o.size for o in outs)
    return pl.pallas_call(
        kernel,
        out_shape=outs,
        in_specs=[SM] + [VM] * (len(args) - 1),
        out_specs=[VM] * len(outs),
        scratch_shapes=scratch,
        compiler_params=pltpu.CompilerParams(vmem_limit_bytes=LIMIT),
        cost_estimate=pl.CostEstimate(flops=flops, bytes_accessed=moved, transcendentals=0),
        name=name,
    )(*args)


def ext_ref(planes, rows):
    return pltpu.VMEM((planes, rows // 8, 8, 128), F32)


def fill_band(band):
    row = lax.broadcasted_iota(jnp.int32, (128, 128), 0)
    col = lax.broadcasted_iota(jnp.int32, (128, 128), 1)
    away = jnp.abs(row - col)
    taps = jnp.where(away == 0, -90.0, jnp.where(away == 1, 16.0, jnp.where(away == 2, -1.0, 0.0)))
    band[0:128] = taps.astype(jnp.bfloat16)
    band[128:256] = taps.astype(jnp.bfloat16)


def load(dst, at, src, x, base, width):
    for j in range(width):
        dst[at, j] = src[x, pl.ds(base + j, 8, stride=width), :]


def store(dst, at, src, x, width):
    for j in range(width):
        dst[at, pl.ds(j, 8, stride=width), :] = src[x, j]


def sweep(field, coef, band, first, count, c_first, put):
    width = field.shape[1]
    sub = lax.broadcasted_iota(jnp.int32, (8, 128), 0)
    top, bottom = sub < 1, sub >= 7
    zero = jnp.zeros((8, 128), F32)

    @pl.loop(0, count, step=GROUP)
    def _(k):
        x = first + k
        flat = field[pl.ds(x, GROUP)].reshape(GROUP * width * 8, 128)
        high = flat.astype(jnp.bfloat16)
        rest = flat - high.astype(F32)
        middle = rest.astype(jnp.bfloat16)
        low = (rest - middle.astype(F32)).astype(jnp.bfloat16)
        lanes = jnp.dot(
            jnp.concatenate([high, middle], 1), band[...], preferred_element_type=F32
        ) + jnp.dot(low, band[0:128], preferred_element_type=F32)
        for p in range(GROUP):
            own = [field[x + p, j] for j in range(width)]
            rows = (
                [jnp.where(top, zero, pltpu.roll(own[width - 2], 1, 0)),
                 jnp.where(top, zero, pltpu.roll(own[width - 1], 1, 0))]
                + own
                + [jnp.where(bottom, zero, pltpu.roll(own[0], 7, 0)),
                   jnp.where(bottom, zero, pltpu.roll(own[1], 7, 0))]
            )
            for j in range(width):
                near = (field[x + p - 1, j] + field[x + p + 1, j]) + (rows[j + 1] + rows[j + 3])
                far = (field[x + p - 2, j] + field[x + p + 2, j]) + (rows[j] + rows[j + 4])
                at = (p * width + j) * 8
                total = 16.0 * near - far + lanes[at : at + 8]
                v = own[j]
                put(k + p, j, (v + v) + coef[c_first + k + p, j] * total)


def pulse(rec, x, tick, flag):
    sub = lax.broadcasted_iota(jnp.int32, (8, 128), 0)
    row = rec[x, pl.ds(tick, 1), :] * flag
    return jnp.where(sub < 1, jnp.broadcast_to(row, (8, 128)), 0.0)


def turn(dst, src, planes, scale=None):
    @pl.loop(0, planes)
    def _(x):
        value = src[x].T
        dst[x] = value if scale is None else value * scale


def prepare_now(ids, now, nowt, give):
    n = now.shape[0]
    turn(nowt, now, n)
    start = pl.multiple_of((1 - ids[1]) * (128 - give.shape[1]), 8)

    @pl.loop(0, n)
    def _(x):
        give[x] = nowt[x, pl.ds(start, give.shape[1]), :]


def prepare_rest(ids, old, coef, rec, nowt, oldt, coeft, send_a, send_b):
    n = old.shape[0]
    turn(oldt, old, n)
    turn(coeft, coef, n, 1.0 / 12.0)
    odd = ids[0]

    def pack(send, high):
        def tail(h):
            return jnp.where(high, n - h, 0)

        for k in range(4):
            send[k] = nowt[tail(4) + k]
        for k in range(2):
            send[4 + k] = oldt[tail(2) + k]
        for k in range(HC):
            send[6 + k] = coeft[tail(HC) + k]
        for k in range(HC):
            send[6 + HC, TPAD * k : TPAD * (k + 1), :] = rec[tail(HC) + k]

    pack(send_a, odd == 0)
    pack(send_b, odd == 1)


def place(odd, n, halo, depth):
    after, before = halo + n, halo - depth
    return jnp.where(odd == 0, after, before), jnp.where(odd == 0, before, after)


def first_block(ids, nowt, oldt, coeft, rec, got_a, got_b,
                give, one, was, cfull, rfull, send_a, send_b,
                cur, old, mid, new, cx, band):
    n = nowt.shape[0]
    odd, role = ids[0], ids[1]
    flag = role.astype(F32)
    rows = one.shape[1]
    base = pl.multiple_of(role * (128 - rows), 8)
    other = pl.multiple_of((1 - role) * (128 - rows), 8)
    fill_band(band)

    @pl.loop(0, n)
    def _(x):
        load(cur, x + 4, nowt, x, 0, 16)
        load(old, x + 2, oldt, x, 0, 16)
        load(cx, x + 2, coeft, x, 0, 16)
        was[x + 4] = nowt[x, pl.ds(base, rows), :]
        cfull[x + HC] = coeft[x, pl.ds(base, rows), :]
        rfull[x + HC] = rec[x]

    a4, b4 = place(odd, n, 4, 4)
    a2, b2 = place(odd, n, 2, 2)
    ac, bc = place(odd, n, HC, HC)
    for got, at4, at2, atc, before in ((got_a, a4, a2, ac, odd == 1), (got_b, b4, b2, bc, odd == 0)):
        near_c = 6 + jnp.where(before, HC - 2, 0)
        for k in range(4):
            load(cur, at4 + k, got, k, 0, 16)
            was[at4 + k] = got[k, pl.ds(base, rows), :]
        for k in range(2):
            load(old, at2 + k, got, 4 + k, 0, 16)
            load(cx, at2 + k, got, near_c + k, 0, 16)
        for k in range(HC):
            cfull[atc + k] = got[6 + k, pl.ds(base, rows), :]
            rfull[atc + k] = got[6 + HC, TPAD * k : TPAD * (k + 1), :]

    def put0(x, j, value):
        value = value - old[x, j]
        if j == 0:
            value = value + pulse(rfull, x + HC - 2, 0, flag)
        mid[x, j] = value

    sweep(cur, cx, band, 2, n + 4, 0, put0)

    def put1(x, j, value):
        value = value - cur[x + 4, j]
        if j == 0:
            value = value + pulse(rfull, x + HC, 1, flag)
        new[x, j] = value

    sweep(mid, cx, band, 2, n, 2, put1)

    @pl.loop(0, n)
    def _(x):
        store(nowt, x, new, x, 16)
        one[x] = nowt[x, pl.ds(base, rows), :]
        give[x] = nowt[x, pl.ds(other, rows), :]

    pack_ends(one, send_a, send_b, odd, role)


def pack_ends(field, send_a, send_b, odd, role):
    n = field.shape[0]
    depth, rows = send_a.shape[0], send_a.shape[1]
    base = pl.multiple_of(role * (field.shape[1] - rows), 8)
    high = n - depth
    for send, start in ((send_a, jnp.where(odd == 0, high, 0)), (send_b, jnp.where(odd == 0, 0, high))):

        @pl.loop(0, depth)
        def _(k):
            send[k] = field[start + k, pl.ds(base, rows), :]


def block(rows, steps, tick, lit, fresh, last, shots, ids, *refs):
    it = iter(refs)
    take = lambda count: [next(it) for _ in range(count)]
    u, got_a, got_b, was = take(4)
    was_a, was_b = take(2) if fresh else (None, None)
    cfull, rfull = take(2)
    mates = take(steps) if lit else []
    first_mate = take(1)[0] if lit and fresh else None
    image_in = take(1)[0] if lit and not fresh else None
    inner = take(1)[0] if steps == 2 else None
    out = take(1)[0] if not (lit and last) else None
    send_a, send_b = take(2) if not last else (None, None)
    image = take(1)[0] if lit and not last else None
    pieces = take(shots) if lit and last else []
    cur, old, mid, cx, band = take(5)
    if lit and last:
        out, image = take(2)

    odd, role = ids[0], ids[1]
    n = u.shape[0]
    width = rows // 8
    halo = 4 * steps
    flag = (1 - role).astype(F32)
    fill_band(band)

    def window(ref):
        return pl.multiple_of(role * (ref.shape[1] - rows), 8)

    reach_old = halo - 4
    if fresh:
        @pl.loop(0, n)
        def _(x):
            load(old, x + reach_old, was, x, window(was), width)

        old_a, old_b = place(odd, n, reach_old, reach_old)

        @pl.loop(0, reach_old)
        def _(k):
            load(old, old_a + k, was_a, k, window(was_a), width)
            load(old, old_b + k, was_b, k, window(was_b), width)
    else:
        shift = (was.shape[0] - n) // 2 - reach_old

        @pl.loop(0, n + 2 * reach_old)
        def _(x):
            load(old, x, was, x + shift, window(was), width)

    @pl.loop(0, n + 2 * (halo - 2))
    def _(x):
        load(cx, x, cfull, x + HC - (halo - 2), window(cfull), width)

    @pl.loop(0, n)
    def _(x):
        load(cur, x + halo, u, x, window(u), width)

    at_a, at_b = place(odd, n, halo, halo)

    @pl.loop(0, halo)
    def _(k):
        load(cur, at_a + k, got_a, k, 0, width)
        load(cur, at_b + k, got_b, k, 0, width)

    now, before = cur, old
    results = []
    for s in range(steps):
        reach = halo - 4 * s
        time = tick + 2 * s

        def put_mid(x, j, value):
            if lit and j == 0:
                value = value + pulse(rfull, x + HC - (reach - 2), time + 1, flag)
            mid[x, j] = value

        sweep(now, cx, band, 2, n + 2 * (reach - 2), halo - reach, put_mid)

        def put_new(x, j, value):
            keep = now[x + 4, j]
            value = value - (keep + keep) - before[x, j]
            if lit and j == 0:
                at = x + HC - (reach - 4)
                value = value + (pulse(rfull, at, time, flag) + pulse(rfull, at, time + 2, flag))
            before[x, j] = value

        sweep(mid, cx, band, 2, n + 2 * (reach - 4), halo - reach + 2, put_new)
        results.append(before)
        if s < steps - 1:
            now, before = before, now.at[pl.ds(8, n + 2 * (reach - 8))]

    if steps == 2:
        @pl.loop(0, n + 8)
        def _(x):
            store(inner, x, results[0], x, width)

    @pl.loop(0, n)
    def _(x):
        store(out, x, results[-1], x, width)

    if not last:
        pack_ends(out, send_a, send_b, odd, role)

    if lit:
        half, pairs = 64, n // 2
        mine = ([inner] if steps == 2 else []) + [out]

        @pl.loop(0, pairs)
        def _(k):
            for side in range(2):
                x = k + side * pairs

                def part(ref, extra):
                    start = pl.multiple_of(role * (ref.shape[1] - half), 8)
                    return ref[x + extra, pl.ds(start, half), :]

                total = None
                for field, mate in zip(mine, mates):
                    product = part(field, (field.shape[0] - n) // 2) * part(mate, (mate.shape[0] - n) // 2)
                    total = product if total is None else total + product
                if fresh:
                    total = total + part(u, 0) * part(first_mate, 0)
                else:
                    total = total + image_in[k, side * half : (side + 1) * half, :]
                image[k, side * half : (side + 1) * half, :] = total

        if last:
            piece = 128 // shots
            weight = IMAGE_EVERY / STEPS

            @pl.loop(0, pairs)
            def _(k):
                image[k] = image[k].T * weight
                for index in range(shots):
                    target = jnp.bitwise_xor(ids[2], index)
                    pieces[index][k] = image[k, pl.ds(pl.multiple_of(target * piece, 8), piece), :]


def combine(count, ids, *refs):
    out = refs[count]
    pairs = refs[0].shape[0]

    @pl.loop(0, pairs)
    def _(k):
        total = refs[0][k]
        for index in range(1, count):
            total = total + refs[index][k]
        out[k] = total[:, :64]
        out[k + pairs] = pltpu.roll(total, 64, 1)[:, :64]


def on_device(states, courant, records):
    states, records = states[0, 0], records[0]
    n = courant.shape[0]
    shots, spaces = lax.axis_size("shot"), lax.axis_size("space")
    role, place_x = lax.axis_index("pair"), lax.axis_index("space")
    odd = place_x % 2
    ids = jnp.stack([odd, role, lax.axis_index("shot")]).astype(jnp.int32)
    rec = jnp.pad(jnp.swapaxes(records, 0, 1), ((0, 0), (0, TPAD - STEPS), (0, 0)))

    pairs_a = [(i, i ^ 1) for i in range(spaces)]
    pairs_b = [(i, i + 1) for i in range(1, spaces - 1, 2)]
    pairs_b = pairs_b + [(j, i) for i, j in pairs_b]

    def swap(send_a, send_b):
        got_b = lax.ppermute(send_b, "space", pairs_b)
        return lax.ppermute(send_a, "space", pairs_a), got_b

    def across(value):
        return lax.ppermute(value, "pair", [(0, 1), (1, 0)])

    def ends(value, depth):
        low, high = value[:depth], value[n - depth :]
        high_first = odd == 0
        return jnp.where(high_first, high, low), jnp.where(high_first, low, high)

    wide, mid_rows, thin = 88, 80, 72
    band = pltpu.VMEM((256, 128), jnp.bfloat16)

    nowt, give_now = call(
        prepare_now, (sds(n, 128, 128), sds(n, wide, 128)), [], ids, states[1], name="prepare_now"
    )
    other_was = across(give_now)
    oldt, coeft, send_a, send_b = call(
        prepare_rest,
        (sds(n, 128, 128), sds(n, 128, 128), sds(7 + HC, 128, 128), sds(7 + HC, 128, 128)),
        [], ids, states[0], courant, rec, nowt, name="prepare_rest",
    )
    got_a, got_b = swap(send_a, send_b)
    give_one, one, was, cfull, rfull, send_a, send_b = call(
        first_block,
        (sds(n, wide, 128), sds(n, wide, 128), sds(n + 8, wide, 128), sds(n + 2 * HC, wide, 128),
         sds(n + 2 * HC, TPAD, 128), sds(DEPTH, wide, 128), sds(DEPTH, wide, 128)),
        [ext_ref(n + 8, 128), ext_ref(n + 4, 128), ext_ref(n + 4, 128), ext_ref(n, 128), ext_ref(n + 4, 128), band],
        ids, nowt, oldt, coeft, rec, got_a, got_b, name="first_block",
    )
    other_one = across(give_one)

    def run(rows, steps, tick, lit, fresh, last, depth, *args):
        outs = []
        if steps == 2:
            outs.append(sds(n + 8, rows, 128))
        if not (lit and last):
            outs.append(sds(n, rows, 128))
        if not last:
            outs += [sds(depth, rows - 8, 128)] * 2
        if lit:
            outs += [sds(n // 2, 128 // shots, 128)] * shots if last else [sds(n // 2, 128, 128)]
        halo = 4 * steps
        scratch = [ext_ref(n + 2 * halo, rows), ext_ref(n + 2 * (halo - 4), rows), ext_ref(n + 2 * (halo - 2), rows),
                   ext_ref(n + 2 * (halo - 2), rows), band]
        if lit and last:
            scratch += [pltpu.VMEM((n, rows, 128), F32), pltpu.VMEM((n // 2, 128, 128), F32)]
        kernel = functools.partial(block, rows, steps, tick, lit, fresh, last, shots)
        return call(kernel, tuple(outs), scratch, ids, *args, name=f"{'other' if lit else 'own'}_{tick}")

    got = swap(send_a, send_b)
    three, five, send_a, send_b = run(wide, 2, 1, False, False, False, 8, one, *got, was, cfull, rfull)
    got = swap(send_a, send_b)
    seven, nine, send_a, send_b = run(mid_rows, 2, 5, False, False, False, 4, five, *got, three, cfull, rfull)
    got = swap(send_a, send_b)
    (eleven,) = run(thin, 1, 9, False, False, True, 0, nine, *got, seven, cfull, rfull)

    got_was = swap(*ends(other_was, 4))
    got = swap(*ends(other_one, 8))
    o_three, o_five, send_a, send_b, image = run(
        wide, 2, 1, True, True, False, 8, other_one, *got, other_was, *got_was, cfull, rfull, three, five, one)
    got = swap(send_a, send_b)
    o_seven, o_nine, send_a, send_b, image = run(
        mid_rows, 2, 5, True, False, False, 4, o_five, *got, o_three, cfull, rfull, seven, nine, image)
    got = swap(send_a, send_b)
    pieces = run(thin, 1, 9, True, False, True, 0, o_nine, *got, o_seven, cfull, rfull, eleven, image)

    arrived = [pieces[0]]
    for index in range(1, shots):
        arrived.append(lax.ppermute(pieces[index], "shot", [(i, i ^ index) for i in range(shots)]))
    (result,) = call(
        functools.partial(combine, shots), (sds(n, 128 // shots, 64),), [], ids, *arrived, name="combine"
    )
    return result


def solution(mesh):
    placed = (
        P("shot", "pair", None, "space", None, None),
        P("space", None, None),
        P("shot", None, "space", None),
    )
    return jax.shard_map(
        on_device, mesh=mesh, in_specs=placed, out_specs=P("space", "shot", "pair"), check_vma=False
    )
```

```python
import functools

import jax
import jax.numpy as jnp
from jax import lax
from jax.experimental import pallas as pl
from jax.experimental.pallas import tpu as pltpu
from jax.sharding import PartitionSpec as P


STEPS = 12
IMAGE_EVERY = 2
GROUP = 4
F32 = jnp.float32
VM = pl.BlockSpec(memory_space=pltpu.VMEM)
SM = pl.BlockSpec(memory_space=pltpu.SMEM)
HC = 6
DEPTH = 8
HR = 8


def sds(*shape):
    return jax.ShapeDtypeStruct(shape, F32)


def call(kernel, outs, scratch, *args, limit=8, flops=1):
    moved = sum(4 * a.size for a in args) + sum(4 * o.size for o in outs)
    return pl.pallas_call(
        kernel,
        out_shape=outs,
        in_specs=[SM] + [VM] * (len(args) - 1),
        out_specs=[VM] * len(outs),
        scratch_shapes=scratch,
        compiler_params=pltpu.CompilerParams(vmem_limit_bytes=limit << 20),
        cost_estimate=pl.CostEstimate(flops=flops, bytes_accessed=moved, transcendentals=0),
    )(*args)


def ext_ref(planes, rows):
    return pltpu.VMEM((planes, rows // 8, 8, 128), F32)


def fill_band(band):
    row = lax.broadcasted_iota(jnp.int32, (128, 128), 0)
    col = lax.broadcasted_iota(jnp.int32, (128, 128), 1)
    away = jnp.abs(row - col)
    taps = jnp.where(away == 0, -90.0, jnp.where(away == 1, 16.0, jnp.where(away == 2, -1.0, 0.0)))
    band[0:128] = taps.astype(jnp.bfloat16)
    band[128:256] = taps.astype(jnp.bfloat16)


def load(dst, at, src, x, base, width):
    for j in range(width):
        dst[at, j] = src[x, pl.ds(base + j, 8, stride=width), :]


def store(dst, at, src, x, width):
    for j in range(width):
        dst[at, pl.ds(j, 8, stride=width), :] = src[x, j]


def sweep(field, coef, band, first, count, c_first, put):
    width = field.shape[1]
    sub = lax.broadcasted_iota(jnp.int32, (8, 128), 0)
    top, bottom = sub < 1, sub >= 7
    zero = jnp.zeros((8, 128), F32)

    @pl.loop(0, count, step=GROUP)
    def _(k):
        x = first + k
        flat = field[pl.ds(x, GROUP)].reshape(GROUP * width * 8, 128)
        high = flat.astype(jnp.bfloat16)
        rest = flat - high.astype(F32)
        middle = rest.astype(jnp.bfloat16)
        low = (rest - middle.astype(F32)).astype(jnp.bfloat16)
        lanes = jnp.dot(
            jnp.concatenate([high, middle], 1), band[...], preferred_element_type=F32
        ) + jnp.dot(low, band[0:128], preferred_element_type=F32)
        for p in range(GROUP):
            own = [field[x + p, j] for j in range(width)]
            rows = (
                [jnp.where(top, zero, pltpu.roll(own[width - 2], 1, 0)),
                 jnp.where(top, zero, pltpu.roll(own[width - 1], 1, 0))]
                + own
                + [jnp.where(bottom, zero, pltpu.roll(own[0], 7, 0)),
                   jnp.where(bottom, zero, pltpu.roll(own[1], 7, 0))]
            )
            for j in range(width):
                near = (field[x + p - 1, j] + field[x + p + 1, j]) + (rows[j + 1] + rows[j + 3])
                far = (field[x + p - 2, j] + field[x + p + 2, j]) + (rows[j] + rows[j + 4])
                at = (p * width + j) * 8
                total = 16.0 * near - far + lanes[at : at + 8]
                v = own[j]
                put(k + p, j, (v + v) + coef[c_first + k + p, j] * total)


def pulse(rec, x, tick, flag):
    sub = lax.broadcasted_iota(jnp.int32, (8, 128), 0)
    row = rec[tick, pl.ds(x, 1), :] * flag
    return jnp.where(sub < 1, jnp.broadcast_to(row, (8, 128)), 0.0)


def pack(ids, states, courant, rec, send_a, send_b, sems):
    n = courant.shape[0]
    copies = []
    for index, (send, high) in enumerate(((send_a, ids[0] == 0), (send_b, ids[0] == 1))):
        at = lambda h: jnp.where(high, n - h, 0)
        moves = [
            (states.at[0, 0, 1, pl.ds(at(4), 4)], send.at[pl.ds(0, 4)]),
            (states.at[0, 0, 0, pl.ds(at(2), 2)], send.at[pl.ds(4, 2)]),
            (courant.at[pl.ds(at(HC), HC)], send.at[pl.ds(6, HC)]),
        ]
        first = pl.multiple_of(at(HR), HR)
        for k in range(STEPS):
            send[6 + HC, HR * k : HR * (k + 1), :] = rec[0, k, pl.ds(first, HR), :]
        for k, (source, target) in enumerate(moves):
            copy = pltpu.make_async_copy(source, target, sems.at[index, k])
            copy.start()
            copies.append(copy)
    for copy in copies:
        copy.wait()


def prepare_now(ids, now, nowt, give):
    start = pl.multiple_of((1 - ids[1]) * (128 - give.shape[1]), 8)
    for k in range(GROUP):
        nowt[k] = now[0, 0, 0, k].T
        give[k] = nowt[k, pl.ds(start, give.shape[1]), :]


def prepare_rest(ids, old, coef, oldt, coeft):
    for k in range(GROUP):
        oldt[k] = old[0, 0, 0, k].T
        coeft[k] = coef[k].T * (1.0 / 12.0)


def place(odd, n, halo, depth):
    after, before = halo + n, halo - depth
    return jnp.where(odd == 0, after, before), jnp.where(odd == 0, before, after)


def first_block(ids, nowt, oldt, coeft, rec, got_a, got_b,
                give, one, was_a, was_b, cfull, rfull, send_a, send_b,
                cur, old, mid, new, cx, band, raw_a, raw_b, plain):
    n = nowt.shape[0]
    odd, role = ids[0], ids[1]
    flag = role.astype(F32)
    rows = one.shape[1]
    base = pl.multiple_of(role * (128 - rows), 8)
    other = pl.multiple_of((1 - role) * (128 - rows), 8)
    fill_band(band)

    @pl.loop(0, n)
    def _(x):
        load(cur, x + 4, nowt, x, 0, 16)
        load(old, x + 2, oldt, x, 0, 16)
        load(cx, x + 2, coeft, x, 0, 16)
        cfull[x + HC] = coeft[x, pl.ds(base, rows), :]

    a_rec, b_rec = place(odd, n, HR, HR)
    for k in range(STEPS):
        rfull[k, HR : HR + n, :] = rec[0, k]
        for got, at in ((got_a, a_rec), (got_b, b_rec)):
            rfull[k, pl.ds(pl.multiple_of(at, HR), HR), :] = got[6 + HC, HR * k : HR * (k + 1), :]

    a4, b4 = place(odd, n, 4, 4)
    a2, b2 = place(odd, n, 2, 2)
    ac, bc = place(odd, n, HC, HC)
    for raw, turned, was in ((got_a, raw_a, was_a), (got_b, raw_b, was_b)):
        for k in range(6 + HC):
            value = raw[k].T
            if k < 4:
                was[k] = value
            turned[k] = value if k < 6 else value * (1.0 / 12.0)

    for got, at4, at2, atc, before in ((raw_a, a4, a2, ac, odd == 1), (raw_b, b4, b2, bc, odd == 0)):
        near_c = 6 + jnp.where(before, HC - 2, 0)
        for k in range(4):
            load(cur, at4 + k, got, k, 0, 16)
        for k in range(2):
            load(old, at2 + k, got, 4 + k, 0, 16)
            load(cx, at2 + k, got, near_c + k, 0, 16)
        for k in range(HC):
            cfull[atc + k] = got[6 + k, pl.ds(base, rows), :]

    def put0(x, j, value):
        value = value - old[x, j]
        if j == 0:
            value = value + pulse(rfull, x + HR - 2, 0, flag)
        mid[x, j] = value

    sweep(cur, cx, band, 2, n + 4, 0, put0)

    def put1(x, j, value):
        value = value - cur[x + 4, j]
        if j == 0:
            value = value + pulse(rfull, x + HR, 1, flag)
        new[x, j] = value

    sweep(mid, cx, band, 2, n, 2, put1)

    @pl.loop(0, n)
    def _(x):
        store(plain, x, new, x, 16)
        one[x] = plain[x, pl.ds(base, rows), :]
        give[x] = plain[x, pl.ds(other, rows), :]

    pack_ends(one, send_a, send_b, odd, role)


def pack_ends(field, send_a, send_b, odd, role):
    n = field.shape[0]
    depth, rows = send_a.shape[0], send_a.shape[1]
    base = pl.multiple_of(role * (field.shape[1] - rows), 8)
    high = n - depth
    for send, start in ((send_a, jnp.where(odd == 0, high, 0)), (send_b, jnp.where(odd == 0, 0, high))):

        @pl.loop(0, depth)
        def _(k):
            send[k] = field[start + k, pl.ds(base, rows), :]


def block(rows, steps, tick, lit, fresh, last, shots, ids, *refs):
    it = iter(refs)
    take = lambda count: [next(it) for _ in range(count)]
    u, got_a, got_b, was = take(4)
    was_a, was_b = take(2) if fresh else (None, None)
    cfull, rfull = take(2)
    mates = take(steps) if lit else []
    first_mate = take(1)[0] if lit and fresh else None
    image_in = take(1)[0] if lit and not fresh else None
    inner = take(1)[0] if steps == 2 else None
    out = take(1)[0] if not (lit and last) else None
    send_a, send_b = take(2) if not last else (None, None)
    image = take(1)[0] if lit and not last else None
    pieces = take(shots) if lit and last else []
    cur, old, mid, cx, band = take(5)
    if lit and last:
        out, image = take(2)

    odd, role = ids[0], ids[1]
    n = u.shape[0]
    width = rows // 8
    halo = 4 * steps
    flag = (1 - role).astype(F32)
    fill_band(band)

    def window(ref):
        return pl.multiple_of(role * (ref.shape[1] - rows), 8)

    reach_old = halo - 4
    if fresh:
        @pl.loop(0, n)
        def _(x):
            load(old, x + reach_old, was, x, window(was), width)

        old_a, old_b = place(odd, n, reach_old, reach_old)

        @pl.loop(0, reach_old)
        def _(k):
            load(old, old_a + k, was_a, k, window(was_a), width)
            load(old, old_b + k, was_b, k, window(was_b), width)
    else:
        shift = (was.shape[0] - n) // 2 - reach_old

        @pl.loop(0, n + 2 * reach_old)
        def _(x):
            load(old, x, was, x + shift, window(was), width)

    @pl.loop(0, n + 2 * (halo - 2))
    def _(x):
        load(cx, x, cfull, x + HC - (halo - 2), window(cfull), width)

    @pl.loop(0, n)
    def _(x):
        load(cur, x + halo, u, x, window(u), width)

    at_a, at_b = place(odd, n, halo, halo)

    @pl.loop(0, halo)
    def _(k):
        load(cur, at_a + k, got_a, k, 0, width)
        load(cur, at_b + k, got_b, k, 0, width)

    now, before = cur, old
    results = []
    for s in range(steps):
        reach = halo - 4 * s
        time = tick + 2 * s

        def put_mid(x, j, value):
            if lit and j == 0:
                value = value + pulse(rfull, x + HR - (reach - 2), time + 1, flag)
            mid[x, j] = value

        sweep(now, cx, band, 2, n + 2 * (reach - 2), halo - reach, put_mid)

        def put_new(x, j, value):
            keep = now[x + 4, j]
            value = value - (keep + keep) - before[x, j]
            if lit and j == 0:
                at = x + HR - (reach - 4)
                value = value + (pulse(rfull, at, time, flag) + pulse(rfull, at, time + 2, flag))
            before[x, j] = value

        sweep(mid, cx, band, 2, n + 2 * (reach - 4), halo - reach + 2, put_new)
        results.append(before)
        if s < steps - 1:
            now, before = before, now.at[pl.ds(8, n + 2 * (reach - 8))]

    if steps == 2:
        @pl.loop(0, n + 8)
        def _(x):
            store(inner, x, results[0], x, width)

    @pl.loop(0, n)
    def _(x):
        store(out, x, results[-1], x, width)

    if not last:
        pack_ends(out, send_a, send_b, odd, role)

    if lit:
        half, pairs = 64, n // 2
        mine = ([inner] if steps == 2 else []) + [out]

        @pl.loop(0, pairs)
        def _(k):
            for side in range(2):
                x = k + side * pairs

                def part(ref, extra):
                    start = pl.multiple_of(role * (ref.shape[1] - half), 8)
                    return ref[x + extra, pl.ds(start, half), :]

                total = None
                for field, mate in zip(mine, mates):
                    product = part(field, (field.shape[0] - n) // 2) * part(mate, (mate.shape[0] - n) // 2)
                    total = product if total is None else total + product
                if fresh:
                    total = total + part(u, 0) * part(first_mate, 0)
                else:
                    total = total + image_in[k, side * half : (side + 1) * half, :]
                image[k, side * half : (side + 1) * half, :] = total

        if last:
            piece = 128 // shots
            weight = IMAGE_EVERY / STEPS

            @pl.loop(0, pairs)
            def _(k):
                image[k] = image[k].T * weight
                for index in range(shots):
                    target = jnp.bitwise_xor(ids[2], index)
                    pieces[index][k] = image[k, pl.ds(pl.multiple_of(target * piece, 8), piece), :]


def combine(count, ids, *refs):
    out = refs[count]
    pairs = refs[0].shape[0]

    @pl.loop(0, pairs)
    def _(k):
        total = refs[0][k]
        for index in range(1, count):
            total = total + refs[index][k]
        out[k] = total[:, :64]
        out[k + pairs] = pltpu.roll(total, 64, 1)[:, :64]


def on_device(states, courant, records):
    n = courant.shape[0]
    shots, spaces = lax.axis_size("shot"), lax.axis_size("space")
    role, place_x = lax.axis_index("pair"), lax.axis_index("space")
    odd = place_x % 2
    ids = jnp.stack([odd, role, lax.axis_index("shot")]).astype(jnp.int32)

    pairs_a = [(i, i ^ 1) for i in range(spaces)]
    pairs_b = [(i, i + 1) for i in range(1, spaces - 1, 2)]
    pairs_b = pairs_b + [(j, i) for i, j in pairs_b]

    def swap(send_a, send_b):
        got_b = lax.ppermute(send_b, "space", pairs_b)
        return lax.ppermute(send_a, "space", pairs_a), got_b

    def across(value):
        return lax.ppermute(value, "pair", [(0, 1), (1, 0)])

    def ends(value, depth):
        low, high = value[:depth], value[n - depth :]
        high_first = odd == 0
        return jnp.where(high_first, high, low), jnp.where(high_first, low, high)

    wide, mid_rows, thin = 88, 80, 72
    band = pltpu.VMEM((256, 128), jnp.bfloat16)
    hbm = pl.BlockSpec(memory_space=pltpu.HBM)

    send_a, send_b = pl.pallas_call(
        pack,
        out_shape=(sds(7 + HC, 128, 128),) * 2,
        in_specs=[SM, hbm, hbm, VM],
        out_specs=[VM, VM],
        scratch_shapes=[pltpu.SemaphoreType.DMA((2, 3))],
        compiler_params=pltpu.CompilerParams(vmem_limit_bytes=58 << 20),
        name="pack",
    )(ids, states, courant, records)
    got_a, got_b = swap(send_a, send_b)

    def state_block(index):
        return pl.BlockSpec((1, 1, 1, GROUP, 128, 128), lambda i: (0, 0, index, i, 0, 0))

    def planes(rows):
        return pl.BlockSpec((GROUP, rows, 128), lambda i: (i, 0, 0))

    nowt, give_now = pl.pallas_call(
        prepare_now,
        grid=(n // GROUP,),
        out_shape=(sds(n, 128, 128), sds(n, wide, 128)),
        in_specs=[SM, state_block(1)],
        out_specs=[planes(128), planes(wide)],
        compiler_params=pltpu.CompilerParams(vmem_limit_bytes=6 << 20),
        name="prepare_now",
    )(ids, states)
    other_was = across(give_now)
    oldt, coeft = pl.pallas_call(
        prepare_rest,
        grid=(n // GROUP,),
        out_shape=(sds(n, 128, 128), sds(n, 128, 128)),
        in_specs=[SM, state_block(0), planes(128)],
        out_specs=[planes(128), planes(128)],
        compiler_params=pltpu.CompilerParams(vmem_limit_bytes=6 << 20),
        name="prepare_rest",
    )(ids, states, courant)
    give_one, one, was_a, was_b, cfull, rfull, send_a, send_b = call(
        first_block,
        (sds(n, wide, 128), sds(n, wide, 128), sds(4, 128, 128), sds(4, 128, 128), sds(n + 2 * HC, wide, 128),
         sds(STEPS, n + 2 * HR, 128), sds(DEPTH, wide, 128), sds(DEPTH, wide, 128)),
        [ext_ref(n + 8, 128), ext_ref(n + 4, 128), ext_ref(n + 4, 128), ext_ref(n, 128), ext_ref(n + 4, 128), band]
        + [pltpu.VMEM((6 + HC, 128, 128), F32)] * 2 + [pltpu.VMEM((n, 128, 128), F32)],
        ids, nowt, oldt, coeft, records, got_a, got_b, limit=12,
    )
    other_one = across(give_one)

    def run(rows, steps, tick, lit, fresh, last, depth, *args):
        outs = []
        if steps == 2:
            outs.append(sds(n + 8, rows, 128))
        if not (lit and last):
            outs.append(sds(n, rows, 128))
        if not last:
            outs += [sds(depth, rows - 8, 128)] * 2
        if lit:
            outs += [sds(n // 2, 128 // shots, 128)] * shots if last else [sds(n // 2, 128, 128)]
        halo = 4 * steps
        scratch = [ext_ref(n + 2 * halo, rows), ext_ref(n + 2 * (halo - 4), rows), ext_ref(n + 2 * (halo - 2), rows),
                   ext_ref(n + 2 * (halo - 2), rows), band]
        if lit and last:
            scratch += [pltpu.VMEM((n, rows, 128), F32), pltpu.VMEM((n // 2, 128, 128), F32)]
        kernel = functools.partial(block, rows, steps, tick, lit, fresh, last, shots)
        return call(kernel, tuple(outs), scratch, ids, *args)

    got = swap(send_a, send_b)
    three, five, send_a, send_b = run(wide, 2, 1, False, True, False, 8, one, *got, nowt, was_a, was_b, cfull, rfull)
    got = swap(send_a, send_b)
    seven, nine, send_a, send_b = run(mid_rows, 2, 5, False, False, False, 4, five, *got, three, cfull, rfull)
    got = swap(send_a, send_b)
    (eleven,) = run(thin, 1, 9, False, False, True, 0, nine, *got, seven, cfull, rfull)

    got_was = swap(*ends(other_was, 4))
    got = swap(*ends(other_one, 8))
    o_three, o_five, send_a, send_b, image = run(
        wide, 2, 1, True, True, False, 8, other_one, *got, other_was, *got_was, cfull, rfull, three, five, one)
    got = swap(send_a, send_b)
    o_seven, o_nine, send_a, send_b, image = run(
        mid_rows, 2, 5, True, False, False, 4, o_five, *got, o_three, cfull, rfull, seven, nine, image)
    got = swap(send_a, send_b)
    pieces = run(thin, 1, 9, True, False, True, 0, o_nine, *got, o_seven, cfull, rfull, eleven, image)

    arrived = [pieces[0]]
    for index in range(1, shots):
        arrived.append(lax.ppermute(pieces[index], "shot", [(i, i ^ index) for i in range(shots)]))
    (result,) = call(functools.partial(combine, shots), (sds(n, 128 // shots, 64),), [], ids, *arrived)
    return result


def solution(mesh):
    placed = (
        P("shot", "pair", None, "space", None, None),
        P("space", None, None),
        P("shot", None, "space", None),
    )
    return jax.shard_map(on_device, mesh=mesh, in_specs=placed, out_specs=P("space", "shot", "pair"), check_vma=False)
```

```python
import functools

import jax
import jax.numpy as jnp
from jax import lax
from jax.experimental import pallas as pl
from jax.experimental.pallas import tpu as pltpu
from jax.sharding import PartitionSpec as P


STEPS = 12
IMAGE_EVERY = 2
GROUP = 4
F32 = jnp.float32
VM = pl.BlockSpec(memory_space=pltpu.VMEM)
HC = 6
DEPTH = 8
MORE = 4
HR = 16
REC = 8
PER = 128 // HR
FIRST = REC + -(-STEPS // PER)


def sds(*shape):
    return jax.ShapeDtypeStruct(shape, F32)


def call(kernel, outs, scratch, *args, limit=8, flops=1):
    moved = sum(4 * a.size for a in args) + sum(4 * o.size for o in outs)
    return pl.pallas_call(
        kernel,
        out_shape=outs,
        in_specs=[VM] * len(args),
        out_specs=[VM] * len(outs),
        scratch_shapes=scratch,
        compiler_params=pltpu.CompilerParams(vmem_limit_bytes=limit << 20),
        cost_estimate=pl.CostEstimate(flops=flops, bytes_accessed=moved, transcendentals=0),
    )(*args)


def ext_ref(planes, rows):
    return pltpu.VMEM((planes, rows // 8, 8, 128), F32)


def parity():
    return lax.rem(lax.axis_index("space"), 2)


def fill_band(band):
    row = lax.broadcasted_iota(jnp.int32, (128, 128), 0)
    col = lax.broadcasted_iota(jnp.int32, (128, 128), 1)
    away = jnp.abs(row - col)
    taps = jnp.where(away == 0, -90.0, jnp.where(away == 1, 16.0, jnp.where(away == 2, -1.0, 0.0)))
    band[0:128] = taps.astype(jnp.bfloat16)
    band[128:256] = taps.astype(jnp.bfloat16)


def load(dst, at, src, x, base, width):
    for j in range(width):
        dst[at, j] = src[x, pl.ds(base + j, 8, stride=width), :]


def store(dst, at, src, x, width):
    for j in range(width):
        dst[at, pl.ds(j, 8, stride=width), :] = src[x, j]


def sweep(field, coef, band, first, count, c_first, put):
    width = field.shape[1]
    sub = lax.broadcasted_iota(jnp.int32, (8, 128), 0)
    top, bottom = sub < 1, sub >= 7
    zero = jnp.zeros((8, 128), F32)

    @pl.loop(0, count, step=GROUP)
    def _(k):
        x = first + k
        flat = field[pl.ds(x, GROUP)].reshape(GROUP * width * 8, 128)
        high = flat.astype(jnp.bfloat16)
        rest = flat - high.astype(F32)
        middle = rest.astype(jnp.bfloat16)
        low = (rest - middle.astype(F32)).astype(jnp.bfloat16)
        lanes = jnp.dot(
            jnp.concatenate([high, middle], 1), band[...], preferred_element_type=F32
        ) + jnp.dot(low, band[0:128], preferred_element_type=F32)
        for p in range(GROUP):
            own = [field[x + p, j] for j in range(width)]
            rows = (
                [jnp.where(top, zero, pltpu.roll(own[width - 2], 1, 0)),
                 jnp.where(top, zero, pltpu.roll(own[width - 1], 1, 0))]
                + own
                + [jnp.where(bottom, zero, pltpu.roll(own[0], 7, 0)),
                   jnp.where(bottom, zero, pltpu.roll(own[1], 7, 0))]
            )
            for j in range(width):
                near = (field[x + p - 1, j] + field[x + p + 1, j]) + (rows[j + 1] + rows[j + 3])
                far = (field[x + p - 2, j] + field[x + p + 2, j]) + (rows[j] + rows[j + 4])
                at = (p * width + j) * 8
                total = 16.0 * near - far + lanes[at : at + 8]
                v = own[j]
                put(k + p, j, v, coef[c_first + k + p, j] * total)


def pulse(rec, x, tick, flag):
    sub = lax.broadcasted_iota(jnp.int32, (8, 128), 0)
    row = rec[tick, pl.ds(x, 1), :] * flag
    return jnp.where(sub < 1, jnp.broadcast_to(row, (8, 128)), 0.0)


def pack(states, courant, rec, send_a, send_b, sems):
    n = courant.shape[0]
    odd = parity()
    copies = []
    for index, (send, high) in enumerate(((send_a, odd == 0), (send_b, odd == 1))):
        at = lambda h: jnp.where(high, n - h, 0)
        moves = [
            (states.at[0, 0, 1, pl.ds(at(4), 4)], send.at[pl.ds(0, 4)]),
            (states.at[0, 0, 0, pl.ds(at(2), 2)], send.at[pl.ds(4, 2)]),
            (courant.at[pl.ds(at(2), 2)], send.at[pl.ds(6, 2)]),
        ]
        first = pl.multiple_of(at(HR), HR)
        for k in range(STEPS):
            send[REC + k // PER, HR * (k % PER) : HR * (k % PER + 1), :] = rec[0, k, pl.ds(first, HR), :]
        for k, (source, target) in enumerate(moves):
            copy = pltpu.make_async_copy(source, target, sems.at[index, k])
            copy.start()
            copies.append(copy)
    for copy in copies:
        copy.wait()


def prepare_now(now, nowt, give):
    start = pl.multiple_of((1 - lax.axis_index("pair")) * (128 - give.shape[1]), 8)
    for k in range(GROUP):
        nowt[k] = now[0, 0, 0, k].T
        give[k] = nowt[k, pl.ds(start, give.shape[1]), :]


def prepare_rest(old, coef, oldt, coeft):
    for k in range(GROUP):
        oldt[k] = old[0, 0, 0, k].T
        coeft[k] = coef[k].T * (1.0 / 12.0)


def place(odd, n, halo, depth):
    after, before = halo + n, halo - depth
    return jnp.where(odd == 0, after, before), jnp.where(odd == 0, before, after)


def first_block(nowt, oldt, coeft, rec, got_a, got_b,
                give, one, near, rfull, send_a, send_b,
                cur, old, mid, new, cx, band, raw_a, raw_b, plain):
    n = nowt.shape[0]
    odd, role = parity(), lax.axis_index("pair")
    flag = role.astype(F32)
    rows = one.shape[1]
    base = pl.multiple_of(role * (128 - rows), 8)
    other = pl.multiple_of((1 - role) * (128 - rows), 8)
    fill_band(band)

    @pl.loop(0, n)
    def _(x):
        load(cur, x + 4, nowt, x, 0, 16)
        load(old, x + 2, oldt, x, 0, 16)
        load(cx, x + 2, coeft, x, 0, 16)
        near[x + 2] = coeft[x, pl.ds(base, rows), :]

    for raw, turned in ((got_a, raw_a), (got_b, raw_b)):
        for k in range(REC):
            value = raw[k].T
            turned[k] = value if k < 6 else value * (1.0 / 12.0)

    a_rec, b_rec = place(odd, n, HR, HR)
    for k in range(STEPS):
        rfull[k, HR : HR + n, :] = rec[0, k]
        for got, at in ((got_a, a_rec), (got_b, b_rec)):
            piece = got[REC + k // PER, HR * (k % PER) : HR * (k % PER + 1), :]
            rfull[k, pl.ds(pl.multiple_of(at, 8), HR), :] = piece

    a4, b4 = place(odd, n, 4, 4)
    a2, b2 = place(odd, n, 2, 2)
    for got, at4, at2, spot in ((raw_a, a4, a2, n + 4), (raw_b, b4, b2, n + 8)):
        for k in range(4):
            load(cur, at4 + k, got, k, 0, 16)
            near[spot + k] = got[k, pl.ds(base, rows), :]
        for k in range(2):
            load(old, at2 + k, got, 4 + k, 0, 16)
            load(cx, at2 + k, got, 6 + k, 0, 16)
            near[at2 + k] = got[6 + k, pl.ds(base, rows), :]

    def put0(x, j, v, change):
        value = (v + v) - old[x, j] + change
        if j == 0:
            value = value + pulse(rfull, x + HR - 2, 0, flag)
        mid[x, j] = value

    sweep(cur, cx, band, 2, n + 4, 0, put0)

    def put1(x, j, v, change):
        value = (v + v) - cur[x + 4, j] + change
        if j == 0:
            value = value + pulse(rfull, x + HR, 1, flag)
        new[x, j] = value

    sweep(mid, cx, band, 2, n, 2, put1)

    @pl.loop(0, n)
    def _(x):
        store(plain, x, new, x, 16)
        one[x] = plain[x, pl.ds(base, rows), :]
        give[x] = plain[x, pl.ds(other, rows), :]

    pack_ends(one, send_a, send_b, odd, role, DEPTH)
    for send, high in ((send_a, odd == 0), (send_b, odd == 1)):
        start = jnp.where(high, n - HC, 2) + 2
        for k in range(HC - 2):
            send[DEPTH + k] = near[start + k]


def pack_ends(field, send_a, send_b, odd, role, depth):
    n, rows = field.shape[0], send_a.shape[1]
    base = pl.multiple_of(role * (field.shape[1] - rows), 8)
    high = n - depth
    for send, start in ((send_a, jnp.where(odd == 0, high, 0)), (send_b, jnp.where(odd == 0, 0, high))):

        @pl.loop(0, depth)
        def _(k):
            send[k] = field[start + k, pl.ds(base, rows), :]


def block(rows, steps, tick, lit, fresh, last, shots, *refs):
    it = iter(refs)
    take = lambda count: [next(it) for _ in range(count)]
    u, got_a, got_b, was, coef, rfull = take(6)
    was_a, was_b = take(2) if fresh and lit else (None, None)
    mates = take(steps) if lit else []
    first_mate = take(1)[0] if lit and fresh else None
    image_in = take(1)[0] if lit and not fresh else None
    inner = take(1)[0] if steps > 1 else None
    out = take(1)[0] if not (lit and last) else None
    send_a, send_b = take(2) if not last else (None, None)
    whole = take(1)[0] if fresh and not lit else coef
    image = take(1)[0] if lit and not last else None
    pieces = take(shots) if lit and last else []
    cur, old, mid, cx, band = take(5)
    third = take(1)[0] if steps == 3 else None
    if lit and last:
        out, image = take(2)

    odd, role = parity(), lax.axis_index("pair")
    n = u.shape[0]
    width = rows // 8
    halo = 4 * steps
    flag = (1 - role).astype(F32)
    fill_band(band)

    def window(ref):
        return pl.multiple_of(role * (ref.shape[1] - rows), 8)

    if fresh and not lit:
        was_a, was_b = coef.at[pl.ds(n + 4, 4)], coef.at[pl.ds(n + 8, 4)]

        @pl.loop(0, n + 4)
        def _(x):
            whole[x + HC - 2] = coef[x]

        at_a, at_b = place(odd, n + 4, HC - 2, HC - 2)
        for k in range(HC - 2):
            whole[at_a + k] = got_a[DEPTH + k]
            whole[at_b + k] = got_b[DEPTH + k]

    reach_old = halo - 4
    if fresh:
        @pl.loop(0, n)
        def _(x):
            load(old, x + reach_old, was, x, window(was), width)

        old_a, old_b = place(odd, n, reach_old, reach_old)

        @pl.loop(0, reach_old)
        def _(k):
            load(old, old_a + k, was_a, k, window(was_a), width)
            load(old, old_b + k, was_b, k, window(was_b), width)
    else:
        shift = (was.shape[0] - n) // 2 - reach_old

        @pl.loop(0, n + 2 * reach_old)
        def _(x):
            load(old, x, was, x + shift, window(was), width)

    beyond = max(halo - 2 - HC, 0)

    @pl.loop(0, n + 2 * min(halo - 2, HC))
    def _(x):
        load(cx, x + beyond, whole, x + max(HC - (halo - 2), 0), window(whole), width)

    if beyond:
        at_a, at_b = place(odd, n + 2 * HC, beyond, beyond)

        @pl.loop(0, beyond)
        def _(k):
            load(cx, at_a + k, was_a, reach_old + k, window(was_a), width)
            load(cx, at_b + k, was_b, reach_old + k, window(was_b), width)

    @pl.loop(0, n)
    def _(x):
        load(cur, x + halo, u, x, window(u), width)

    at_a, at_b = place(odd, n, halo, halo)

    @pl.loop(0, halo)
    def _(k):
        load(cur, at_a + k, got_a, k, 0, width)
        load(cur, at_b + k, got_b, k, 0, width)

    now, before = cur, old
    for s in range(steps):
        reach = halo - 4 * s
        time = tick + 2 * s

        def put_mid(x, j, v, change):
            value = (v + v) + change
            if lit and j == 0:
                value = value + pulse(rfull, x + HR - (reach - 2), time + 1, flag)
            mid[x, j] = value

        sweep(now, cx, band, 2, n + 2 * (reach - 2), halo - reach, put_mid)

        def put_new(x, j, v, change):
            gain = v - now[x + 4, j]
            value = (gain + gain) - before[x, j] + change
            if lit and j == 0:
                at = x + HR - (reach - 4)
                value = value + (pulse(rfull, at, time, flag) + pulse(rfull, at, time + 2, flag))
            before[x, j] = value

        sweep(mid, cx, band, 2, n + 2 * (reach - 4), halo - reach + 2, put_new)
        target = (third, inner, out)[3 - steps + s]
        skip = (reach - 4) - (target.shape[0] - n) // 2

        @pl.loop(0, target.shape[0])
        def _(x):
            store(target, x, before, x + skip, width)

        if s < steps - 1:
            now, before = before, now.at[pl.ds(8, n + 2 * (reach - 8))]

    if not last:
        pack_ends(out, send_a, send_b, odd, role, send_a.shape[0])

    if lit:
        half, pairs = 64, n // 2
        mine = [third, inner, out][3 - steps :]

        @pl.loop(0, pairs)
        def _(k):
            for side in range(2):
                x = k + side * pairs

                def part(ref, extra):
                    start = pl.multiple_of(role * (ref.shape[1] - half), 8)
                    return ref[x + extra, pl.ds(start, half), :]

                total = None
                for field, mate in zip(mine, mates):
                    product = part(field, (field.shape[0] - n) // 2) * part(mate, (mate.shape[0] - n) // 2)
                    total = product if total is None else total + product
                if fresh:
                    total = total + part(u, 0) * part(first_mate, 0)
                else:
                    total = total + image_in[k, side * half : (side + 1) * half, :]
                image[k, side * half : (side + 1) * half, :] = total

        if last:
            piece = 128 // shots
            weight = IMAGE_EVERY / STEPS

            @pl.loop(0, pairs)
            def _(k):
                image[k] = image[k].T * weight
                for index in range(shots):
                    target = jnp.bitwise_xor(lax.axis_index("shot"), index)
                    pieces[index][k] = image[k, pl.ds(pl.multiple_of(target * piece, 8), piece), :]


def combine(count, *refs):
    out = refs[count]
    pairs = refs[0].shape[0]

    @pl.loop(0, pairs)
    def _(k):
        total = refs[0][k]
        for index in range(1, count):
            total = total + refs[index][k]
        out[k] = total[:, :64]
        out[k + pairs] = pltpu.roll(total, 64, 1)[:, :64]


def on_device(states, courant, records):
    n = courant.shape[0]
    shots, spaces = lax.axis_size("shot"), lax.axis_size("space")
    odd = parity()

    pairs_a = [(i, i ^ 1) for i in range(spaces)]
    pairs_b = [(i, i + 1) for i in range(1, spaces - 1, 2)]
    pairs_b = pairs_b + [(j, i) for i, j in pairs_b]

    def swap(send_a, send_b):
        got_b = lax.ppermute(send_b, "space", pairs_b)
        return lax.ppermute(send_a, "space", pairs_a), got_b

    def across(value):
        return lax.ppermute(value, "pair", [(0, 1), (1, 0)])

    def ends(value, depth, skip=0):
        low, high = value[skip : skip + depth], value[n - skip - depth : n - skip]
        high_first = odd == 0
        return jnp.where(high_first, high, low), jnp.where(high_first, low, high)

    wide, mid_rows, thin = 88, 80, 72
    band = pltpu.VMEM((256, 128), jnp.bfloat16)
    hbm = pl.BlockSpec(memory_space=pltpu.HBM)

    send_a, send_b = pl.pallas_call(
        pack,
        out_shape=(sds(FIRST, 128, 128),) * 2,
        in_specs=[hbm, hbm, VM],
        out_specs=[VM, VM],
        scratch_shapes=[pltpu.SemaphoreType.DMA((2, 3))],
        compiler_params=pltpu.CompilerParams(vmem_limit_bytes=58 << 20),
        name="pack",
    )(states, courant, records)
    got_a, got_b = swap(send_a, send_b)

    def state_block(index):
        return pl.BlockSpec((1, 1, 1, GROUP, 128, 128), lambda i: (0, 0, index, i, 0, 0))

    def planes(rows):
        return pl.BlockSpec((GROUP, rows, 128), lambda i: (i, 0, 0))

    nowt, give_now = pl.pallas_call(
        prepare_now,
        grid=(n // GROUP,),
        out_shape=(sds(n, 128, 128), sds(n, wide, 128)),
        in_specs=[state_block(1)],
        out_specs=[planes(128), planes(wide)],
        compiler_params=pltpu.CompilerParams(vmem_limit_bytes=6 << 20),
        name="prepare_now",
    )(states)
    other_was = across(give_now)
    oldt, coeft = pl.pallas_call(
        prepare_rest,
        grid=(n // GROUP,),
        out_shape=(sds(n, 128, 128), sds(n, 128, 128)),
        in_specs=[state_block(0), planes(128)],
        out_specs=[planes(128), planes(128)],
        compiler_params=pltpu.CompilerParams(vmem_limit_bytes=6 << 20),
        name="prepare_rest",
    )(states, courant)
    give_one, one, near, rfull, send_a, send_b = call(
        first_block,
        (sds(n, wide, 128), sds(n, wide, 128), sds(n + 12, wide, 128), sds(STEPS, n + 2 * HR, 128),
         sds(DEPTH + HC - 2, wide, 128), sds(DEPTH + HC - 2, wide, 128)),
        [ext_ref(n + 8, 128), ext_ref(n + 4, 128), ext_ref(n + 4, 128), ext_ref(n, 128), ext_ref(n + 4, 128), band]
        + [pltpu.VMEM((REC, 128, 128), F32)] * 2 + [pltpu.VMEM((n, 128, 128), F32)],
        nowt, oldt, coeft, records, got_a, got_b, limit=12,
    )
    other_one = across(give_one)

    def run(rows, steps, tick, lit, fresh, last, depth, after, *args):
        outs = []
        if steps > 1:
            outs.append(sds(n + 8, rows, 128))
        if not (lit and last):
            outs.append(sds(n, rows, 128))
        if not last:
            outs += [sds(depth, after, 128)] * 2
        if fresh and not lit:
            outs.append(sds(n + 2 * HC, rows, 128))
        if lit:
            outs += [sds(n // 2, 128 // shots, 128)] * shots if last else [sds(n // 2, 128, 128)]
        halo = 4 * steps
        scratch = [ext_ref(n + 2 * halo, rows), ext_ref(n + 2 * (halo - 4), rows), ext_ref(n + 2 * (halo - 2), rows),
                   ext_ref(n + 2 * (halo - 2), rows), band]
        if steps == 3:
            scratch.append(pltpu.VMEM((n, rows, 128), F32))
        if lit and last:
            scratch += [pltpu.VMEM((n, rows, 128), F32), pltpu.VMEM((n // 2, 128, 128), F32)]
        kernel = functools.partial(block, rows, steps, tick, lit, fresh, last, shots)
        return call(kernel, tuple(outs), scratch, *args, limit=10)

    got = swap(send_a, send_b)
    three, five, send_a, send_b, cfull = run(
        wide, 2, 1, False, True, False, 8, mid_rows, one, *got, nowt, near, rfull)
    got = swap(send_a, send_b)
    seven, nine, send_a, send_b = run(
        mid_rows, 2, 5, False, False, False, 4, thin, five, *got, three, cfull, rfull)
    got = swap(send_a, send_b)
    (eleven,) = run(thin, 1, 9, False, False, True, 0, 0, nine, *got, seven, cfull, rfull)

    was_ends, coef_ends = ends(other_was, 8), ends(near[2 : 2 + n], MORE, HC)
    got_was = swap(*(jnp.concatenate(pair) for pair in zip(was_ends, coef_ends)))
    got = swap(*ends(other_one, 12))
    o_five, o_seven, send_a, send_b, image = run(
        wide, 3, 1, True, True, False, 8, thin,
        other_one, *got, other_was, cfull, rfull, *got_was, three, five, seven, one)
    got = swap(send_a, send_b)
    _, *pieces = run(
        thin, 2, 7, True, False, True, 0, 0, o_seven, *got, o_five, cfull, rfull, nine, eleven, image)

    arrived = [pieces[0]]
    for index in range(1, shots):
        arrived.append(lax.ppermute(pieces[index], "shot", [(i, i ^ index) for i in range(shots)]))
    (result,) = call(functools.partial(combine, shots), (sds(n, 128 // shots, 64),), [], *arrived)
    return result


def solution(mesh):
    placed = (
        P("shot", "pair", None, "space", None, None),
        P("space", None, None),
        P("shot", None, "space", None),
    )
    return jax.shard_map(on_device, mesh=mesh, in_specs=placed, out_specs=P("space", "shot", "pair"), check_vma=False)
```

```python
import functools

import jax
import jax.numpy as jnp
from jax import lax
from jax.experimental import pallas as pl
from jax.experimental.pallas import tpu as pltpu
from jax.sharding import PartitionSpec as P


STEPS = 12
IMAGE_EVERY = 2
GROUP = 4
F32 = jnp.float32
VM = pl.BlockSpec(memory_space=pltpu.VMEM)
HC = 6
DEPTH = 8
MORE = 4
HR = 16
REC = 8
PER = 128 // HR
FIRST = REC + -(-STEPS // PER)


def sds(*shape):
    return jax.ShapeDtypeStruct(shape, F32)


def call(kernel, outs, scratch, *args, limit=8, flops=1):
    moved = sum(4 * a.size for a in args) + sum(4 * o.size for o in outs)
    return pl.pallas_call(
        kernel,
        out_shape=outs,
        in_specs=[VM] * len(args),
        out_specs=[VM] * len(outs),
        scratch_shapes=scratch,
        compiler_params=pltpu.CompilerParams(vmem_limit_bytes=limit << 20),
        cost_estimate=pl.CostEstimate(flops=flops, bytes_accessed=moved, transcendentals=0),
    )(*args)


def ext_ref(planes, rows):
    return pltpu.VMEM((planes, rows // 8, 8, 128), F32)


def parity():
    return lax.rem(lax.axis_index("space"), 2)


def fill_band(band):
    row = lax.broadcasted_iota(jnp.int32, (128, 128), 0)
    col = lax.broadcasted_iota(jnp.int32, (128, 128), 1)
    away = jnp.abs(row - col)
    taps = jnp.where(away == 0, -90.0, jnp.where(away == 1, 16.0, jnp.where(away == 2, -1.0, 0.0)))
    band[0:128] = taps.astype(jnp.bfloat16)
    band[128:256] = taps.astype(jnp.bfloat16)


def load(dst, at, src, x, base, width):
    for j in range(width):
        dst[at, j] = src[x, pl.ds(base + j, 8, stride=width), :]


def store(dst, at, src, x, width):
    for j in range(width):
        dst[at, pl.ds(j, 8, stride=width), :] = src[x, j]


def sweep(field, coef, band, first, count, c_first, put):
    width = field.shape[1]
    sub = lax.broadcasted_iota(jnp.int32, (8, 128), 0)
    top, bottom = sub < 1, sub >= 7
    zero = jnp.zeros((8, 128), F32)

    @pl.loop(0, count, step=GROUP, unroll=True)
    def _(k):
        x = first + k
        flat = field[pl.ds(x, GROUP)].reshape(GROUP * width * 8, 128)
        high = flat.astype(jnp.bfloat16)
        rest = flat - high.astype(F32)
        middle = rest.astype(jnp.bfloat16)
        low = (rest - middle.astype(F32)).astype(jnp.bfloat16)
        lanes = jnp.dot(
            jnp.concatenate([high, middle], 1), band[...], preferred_element_type=F32
        ) + jnp.dot(low, band[0:128], preferred_element_type=F32)
        for p in range(GROUP):
            own = [field[x + p, j] for j in range(width)]
            rows = (
                [jnp.where(top, zero, pltpu.roll(own[width - 2], 1, 0)),
                 jnp.where(top, zero, pltpu.roll(own[width - 1], 1, 0))]
                + own
                + [jnp.where(bottom, zero, pltpu.roll(own[0], 7, 0)),
                   jnp.where(bottom, zero, pltpu.roll(own[1], 7, 0))]
            )
            for j in range(width):
                near = (field[x + p - 1, j] + field[x + p + 1, j]) + (rows[j + 1] + rows[j + 3])
                far = (field[x + p - 2, j] + field[x + p + 2, j]) + (rows[j] + rows[j + 4])
                at = (p * width + j) * 8
                total = 16.0 * near - far + lanes[at : at + 8]
                v = own[j]
                put(k + p, j, v, coef[c_first + k + p, j] * total)


def pulse(rec, x, tick, flag):
    sub = lax.broadcasted_iota(jnp.int32, (8, 128), 0)
    row = rec[tick, pl.ds(x, 1), :] * flag
    return jnp.where(sub < 1, jnp.broadcast_to(row, (8, 128)), 0.0)


def pack(states, courant, rec, send_a, send_b, held_a, held_b, sems):
    n = courant.shape[0]
    odd = parity()
    copies = []
    for index, (send, held, high) in enumerate(((send_a, held_a, odd == 0), (send_b, held_b, odd == 1))):
        at = lambda h: jnp.where(high, n - h, 0)
        moves = (
            (states.at[0, 0, 1, pl.ds(at(4), 4)], 0, 4),
            (states.at[0, 0, 0, pl.ds(at(2), 2)], 4, 2),
            (courant.at[pl.ds(at(2), 2)], 6, 2),
        )
        for k, (source, start, count) in enumerate(moves):
            part = held.at[pl.ds(start, count)]
            come = pltpu.make_async_copy(source, part, sems.at[index, 0, k])
            come.start()
            leave = pltpu.make_async_copy(part, send.at[pl.ds(start, count)], sems.at[index, 1, k])
            copies.append((come, leave))
        first = pl.multiple_of(at(HR), HR)
        for k in range(STEPS):
            held[REC + k // PER, HR * (k % PER) : HR * (k % PER + 1), :] = rec[0, k, pl.ds(first, HR), :]
        tail = pl.ds(REC, FIRST - REC)
        copies.append((None, pltpu.make_async_copy(held.at[tail], send.at[tail], sems.at[index, 1, 3])))
    for come, leave in copies:
        if come is not None:
            come.wait()
        leave.start()
    for _, leave in copies:
        leave.wait()


def prepare_now(now, nowt, give):
    start = pl.multiple_of((1 - lax.axis_index("pair")) * (128 - give.shape[1]), 8)
    for k in range(GROUP):
        nowt[k] = now[0, 0, 0, k].T
        give[k] = nowt[k, pl.ds(start, give.shape[1]), :]


def prepare_rest(old, coef, oldt, coeft):
    for k in range(GROUP):
        oldt[k] = old[0, 0, 0, k].T
        coeft[k] = coef[k].T * (1.0 / 12.0)


def place(odd, n, halo, depth):
    after, before = halo + n, halo - depth
    return jnp.where(odd == 0, after, before), jnp.where(odd == 0, before, after)


def first_block(nowt, oldt, coeft, rec, got_a, got_b,
                give, one, rfull, send_a, send_b,
                cur, old, mid, new, cx, band, raw_a, raw_b, plain):
    n = nowt.shape[0]
    odd, role = parity(), lax.axis_index("pair")
    flag = role.astype(F32)
    rows = one.shape[1]
    base = pl.multiple_of(role * (128 - rows), 8)
    other = pl.multiple_of((1 - role) * (128 - rows), 8)
    fill_band(band)

    @pl.loop(0, n, unroll=4)
    def _(x):
        load(cur, x + 4, nowt, x, 0, 16)
        load(old, x + 2, oldt, x, 0, 16)
        load(cx, x + 2, coeft, x, 0, 16)

    for raw, turned in ((got_a, raw_a), (got_b, raw_b)):
        for k in range(REC):
            value = raw[k].T
            turned[k] = value if k < 6 else value * (1.0 / 12.0)

    a_rec, b_rec = place(odd, n, HR, HR)
    for k in range(STEPS):
        rfull[k, HR : HR + n, :] = rec[0, k]
        for got, at in ((got_a, a_rec), (got_b, b_rec)):
            piece = got[REC + k // PER, HR * (k % PER) : HR * (k % PER + 1), :]
            rfull[k, pl.ds(pl.multiple_of(at, 8), HR), :] = piece

    a4, b4 = place(odd, n, 4, 4)
    a2, b2 = place(odd, n, 2, 2)
    for got, at4, at2 in ((raw_a, a4, a2), (raw_b, b4, b2)):
        for k in range(4):
            load(cur, at4 + k, got, k, 0, 16)
        for k in range(2):
            load(old, at2 + k, got, 4 + k, 0, 16)
            load(cx, at2 + k, got, 6 + k, 0, 16)

    def put0(x, j, v, change):
        value = (v + v) - old[x, j] + change
        if j == 0:
            value = value + pulse(rfull, x + HR - 2, 0, flag)
        mid[x, j] = value

    sweep(cur, cx, band, 2, n + 4, 0, put0)

    def put1(x, j, v, change):
        value = (v + v) - cur[x + 4, j] + change
        if j == 0:
            value = value + pulse(rfull, x + HR, 1, flag)
        new[x, j] = value

    sweep(mid, cx, band, 2, n, 2, put1)

    @pl.loop(0, n, unroll=4)
    def _(x):
        store(plain, x, new, x, 16)
        one[x] = plain[x, pl.ds(base, rows), :]
        give[x] = plain[x, pl.ds(other, rows), :]

    pack_ends(one, send_a, send_b, odd, role, DEPTH)
    for send, high in ((send_a, odd == 0), (send_b, odd == 1)):
        start = jnp.where(high, n - HC, 2)
        for k in range(HC - 2):
            send[DEPTH + k] = coeft[start + k, pl.ds(base, rows), :]


def pack_ends(field, send_a, send_b, odd, role, depth):
    n, rows = field.shape[0], send_a.shape[1]
    base = pl.multiple_of(role * (field.shape[1] - rows), 8)
    high = n - depth
    for send, start in ((send_a, jnp.where(odd == 0, high, 0)), (send_b, jnp.where(odd == 0, 0, high))):

        @pl.loop(0, depth, unroll=4)
        def _(k):
            send[k] = field[start + k, pl.ds(base, rows), :]


def block(rows, steps, tick, lit, fresh, last, shots, *refs):
    it = iter(refs)
    take = lambda count: [next(it) for _ in range(count)]
    u, got_a, got_b, was, coef, rfull = take(6)
    was_a, was_b = take(2) if fresh else (None, None)
    mates = take(steps) if lit else []
    first_mate = take(1)[0] if lit and fresh else None
    image_in = take(1)[0] if lit and not fresh else None
    inner = take(1)[0] if steps > 1 else None
    out = take(1)[0] if not (lit and last) else None
    send_a, send_b = take(2) if not last else (None, None)
    whole = take(1)[0] if fresh and not lit else coef
    image = take(1)[0] if lit and not last else None
    pieces = take(shots) if lit and last else []
    cur, old, mid, cx, band = take(5)
    third = take(1)[0] if steps == 3 else None
    turned = take(2) if fresh and not lit else []
    if lit and last:
        out, image = take(2)

    odd, role = parity(), lax.axis_index("pair")
    n = u.shape[0]
    width = rows // 8
    halo = 4 * steps
    flag = (1 - role).astype(F32)
    fill_band(band)

    def window(ref):
        return pl.multiple_of(role * (ref.shape[1] - rows), 8)

    if fresh and not lit:
        base = window(coef)
        at_a, at_b = place(odd, n, HC, 2)
        far_a, far_b = place(odd, n + 4, HC - 2, HC - 2)

        @pl.loop(0, n, unroll=4)
        def _(x):
            whole[x + HC] = coef[x, pl.ds(base, rows), :]

        for raw, plain, got, at, far in (
            (was_a, turned[0], got_a, at_a, far_a), (was_b, turned[1], got_b, at_b, far_b)
        ):
            for k in range(4):
                plain[k] = raw[k].T
            for k in range(2):
                plain[4 + k] = raw[6 + k].T * (1.0 / 12.0)
                whole[at + k] = plain[4 + k, pl.ds(base, rows), :]
            for k in range(HC - 2):
                whole[far + k] = got[DEPTH + k]
        was_a, was_b = turned

    reach_old = halo - 4
    if fresh:
        @pl.loop(0, n, unroll=4)
        def _(x):
            load(old, x + reach_old, was, x, window(was), width)

        old_a, old_b = place(odd, n, reach_old, reach_old)

        @pl.loop(0, reach_old, unroll=4)
        def _(k):
            load(old, old_a + k, was_a, k, window(was_a), width)
            load(old, old_b + k, was_b, k, window(was_b), width)
    else:
        shift = (was.shape[0] - n) // 2 - reach_old

        @pl.loop(0, n + 2 * reach_old, unroll=4)
        def _(x):
            load(old, x, was, x + shift, window(was), width)

    beyond = max(halo - 2 - HC, 0)

    @pl.loop(0, n + 2 * min(halo - 2, HC), unroll=4)
    def _(x):
        load(cx, x + beyond, whole, x + max(HC - (halo - 2), 0), window(whole), width)

    if beyond:
        at_a, at_b = place(odd, n + 2 * HC, beyond, beyond)

        @pl.loop(0, beyond, unroll=4)
        def _(k):
            load(cx, at_a + k, was_a, reach_old + k, window(was_a), width)
            load(cx, at_b + k, was_b, reach_old + k, window(was_b), width)

    @pl.loop(0, n, unroll=4)
    def _(x):
        load(cur, x + halo, u, x, window(u), width)

    at_a, at_b = place(odd, n, halo, halo)

    @pl.loop(0, halo, unroll=4)
    def _(k):
        load(cur, at_a + k, got_a, k, 0, width)
        load(cur, at_b + k, got_b, k, 0, width)

    now, before = cur, old
    for s in range(steps):
        reach = halo - 4 * s
        time = tick + 2 * s

        def put_mid(x, j, v, change):
            value = (v + v) + change
            if lit and j == 0:
                value = value + pulse(rfull, x + HR - (reach - 2), time + 1, flag)
            mid[x, j] = value

        sweep(now, cx, band, 2, n + 2 * (reach - 2), halo - reach, put_mid)

        def put_new(x, j, v, change):
            gain = v - now[x + 4, j]
            value = (gain + gain) - before[x, j] + change
            if lit and j == 0:
                at = x + HR - (reach - 4)
                value = value + (pulse(rfull, at, time, flag) + pulse(rfull, at, time + 2, flag))
            before[x, j] = value

        sweep(mid, cx, band, 2, n + 2 * (reach - 4), halo - reach + 2, put_new)
        target = (third, inner, out)[3 - steps + s]
        skip = (reach - 4) - (target.shape[0] - n) // 2

        @pl.loop(0, target.shape[0], unroll=4)
        def _(x):
            store(target, x, before, x + skip, width)

        if s < steps - 1:
            now, before = before, now.at[pl.ds(8, n + 2 * (reach - 8))]

    if not last:
        pack_ends(out, send_a, send_b, odd, role, send_a.shape[0])

    if lit:
        half, pairs = 64, n // 2
        mine = [third, inner, out][3 - steps :]

        @pl.loop(0, pairs, unroll=4)
        def _(k):
            for side in range(2):
                x = k + side * pairs

                def part(ref, extra):
                    start = pl.multiple_of(role * (ref.shape[1] - half), 8)
                    return ref[x + extra, pl.ds(start, half), :]

                total = None
                for field, mate in zip(mine, mates):
                    product = part(field, (field.shape[0] - n) // 2) * part(mate, (mate.shape[0] - n) // 2)
                    total = product if total is None else total + product
                if fresh:
                    total = total + part(u, 0) * part(first_mate, 0)
                else:
                    total = total + image_in[k, side * half : (side + 1) * half, :]
                image[k, side * half : (side + 1) * half, :] = total

        if last:
            piece = 128 // shots
            weight = IMAGE_EVERY / STEPS

            @pl.loop(0, pairs, unroll=4)
            def _(k):
                image[k] = image[k].T * weight
                for index in range(shots):
                    target = jnp.bitwise_xor(lax.axis_index("shot"), index)
                    pieces[index][k] = image[k, pl.ds(pl.multiple_of(target * piece, 8), piece), :]


def ends(field, *refs):
    *coef, send_a, send_b = refs
    odd, role = parity(), lax.axis_index("pair")
    n, rows = field.shape[0], field.shape[1]
    depth = send_a.shape[0] - MORE * len(coef)
    pack_ends(field, send_a, send_b, odd, role, depth)
    if coef:
        base = pl.multiple_of(role * (128 - rows), 8)
        for send, high in ((send_a, odd == 0), (send_b, odd == 1)):
            start = jnp.where(high, n - HC - MORE, HC)
            for k in range(MORE):
                send[depth + k] = coef[0][start + k, pl.ds(base, rows), :]


def combine(count, *refs):
    out = refs[count]
    pairs = refs[0].shape[0]

    @pl.loop(0, pairs, unroll=4)
    def _(k):
        total = refs[0][k]
        for index in range(1, count):
            total = total + refs[index][k]
        out[k] = total[:, :64]
        out[k + pairs] = pltpu.roll(total, 64, 1)[:, :64]


def on_device(states, courant, records):
    n = courant.shape[0]
    shots, spaces = lax.axis_size("shot"), lax.axis_size("space")
    odd = parity()

    pairs_a = [(i, i ^ 1) for i in range(spaces)]
    pairs_b = [(i, i + 1) for i in range(1, spaces - 1, 2)]
    pairs_b = pairs_b + [(j, i) for i, j in pairs_b]

    def swap(send_a, send_b):
        got_b = lax.ppermute(send_b, "space", pairs_b)
        return lax.ppermute(send_a, "space", pairs_a), got_b

    def across(value):
        return lax.ppermute(value, "pair", [(0, 1), (1, 0)])

    wide, mid_rows, thin = 88, 80, 72
    band = pltpu.VMEM((256, 128), jnp.bfloat16)
    hbm = pl.BlockSpec(memory_space=pltpu.HBM)

    send_a, send_b = pl.pallas_call(
        pack,
        out_shape=(sds(FIRST, 128, 128),) * 2,
        in_specs=[hbm, hbm, VM],
        out_specs=[hbm, hbm],
        scratch_shapes=[pltpu.VMEM((FIRST, 128, 128), F32)] * 2 + [pltpu.SemaphoreType.DMA((2, 2, 4))],
        compiler_params=pltpu.CompilerParams(vmem_limit_bytes=58 << 20),
        name="pack",
    )(states, courant, records)
    first_a, first_b = swap(send_a, send_b)

    def state_block(index):
        return pl.BlockSpec((1, 1, 1, GROUP, 128, 128), lambda i: (0, 0, index, i, 0, 0))

    def planes(rows):
        return pl.BlockSpec((GROUP, rows, 128), lambda i: (i, 0, 0))

    nowt, give_now = pl.pallas_call(
        prepare_now,
        grid=(n // GROUP,),
        out_shape=(sds(n, 128, 128), sds(n, wide, 128)),
        in_specs=[state_block(1)],
        out_specs=[planes(128), planes(wide)],
        compiler_params=pltpu.CompilerParams(vmem_limit_bytes=6 << 20),
        name="prepare_now",
    )(states)
    other_was = across(give_now)
    oldt, coeft = pl.pallas_call(
        prepare_rest,
        grid=(n // GROUP,),
        out_shape=(sds(n, 128, 128), sds(n, 128, 128)),
        in_specs=[state_block(0), planes(128)],
        out_specs=[planes(128), planes(128)],
        compiler_params=pltpu.CompilerParams(vmem_limit_bytes=6 << 20),
        name="prepare_rest",
    )(states, courant)
    give_one, one, rfull, send_a, send_b = call(
        first_block,
        (sds(n, wide, 128), sds(n, wide, 128), sds(STEPS, n + 2 * HR, 128),
         sds(DEPTH + HC - 2, wide, 128), sds(DEPTH + HC - 2, wide, 128)),
        [ext_ref(n + 8, 128), ext_ref(n + 4, 128), ext_ref(n + 4, 128), ext_ref(n, 128), ext_ref(n + 4, 128), band]
        + [pltpu.VMEM((REC, 128, 128), F32)] * 2 + [pltpu.VMEM((n, 128, 128), F32)],
        nowt, oldt, coeft, records, first_a, first_b, limit=12,
    )
    other_one = across(give_one)

    def run(rows, steps, tick, lit, fresh, last, depth, after, *args):
        outs = []
        if steps > 1:
            outs.append(sds(n + 8, rows, 128))
        if not (lit and last):
            outs.append(sds(n, rows, 128))
        if not last:
            outs += [sds(depth, after, 128)] * 2
        if fresh and not lit:
            outs.append(sds(n + 2 * HC, rows, 128))
        if lit:
            outs += [sds(n // 2, 128 // shots, 128)] * shots if last else [sds(n // 2, 128, 128)]
        halo = 4 * steps
        scratch = [ext_ref(n + 2 * halo, rows), ext_ref(n + 2 * (halo - 4), rows), ext_ref(n + 2 * (halo - 2), rows),
                   ext_ref(n + 2 * (halo - 2), rows), band]
        if steps == 3:
            scratch.append(pltpu.VMEM((n, rows, 128), F32))
        if fresh and not lit:
            scratch += [pltpu.VMEM((6, 128, 128), F32)] * 2
        if lit and last:
            scratch += [pltpu.VMEM((n, rows, 128), F32), pltpu.VMEM((n // 2, 128, 128), F32)]
        kernel = functools.partial(block, rows, steps, tick, lit, fresh, last, shots)
        return call(kernel, tuple(outs), scratch, *args, limit=10)

    got = swap(send_a, send_b)
    three, five, send_a, send_b, cfull = run(
        wide, 2, 1, False, True, False, 8, mid_rows, one, *got, nowt, coeft, rfull, first_a, first_b)
    got = swap(send_a, send_b)
    seven, nine, send_a, send_b = run(
        mid_rows, 2, 5, False, False, False, 4, thin, five, *got, three, cfull, rfull)
    got = swap(send_a, send_b)
    (eleven,) = run(thin, 1, 9, False, False, True, 0, 0, nine, *got, seven, cfull, rfull)

    send_a, send_b = call(ends, (sds(DEPTH + MORE, wide, 128),) * 2, [], other_was, coeft, limit=5)
    got_was = swap(send_a, send_b)
    send_a, send_b = call(ends, (sds(12, wide, 128),) * 2, [], other_one, limit=5)
    got = swap(send_a, send_b)
    o_five, o_seven, send_a, send_b, image = run(
        wide, 3, 1, True, True, False, 8, thin,
        other_one, *got, other_was, cfull, rfull, *got_was, three, five, seven, one)
    got = swap(send_a, send_b)
    _, *pieces = run(
        thin, 2, 7, True, False, True, 0, 0, o_seven, *got, o_five, cfull, rfull, nine, eleven, image)

    arrived = [pieces[0]]
    for index in range(1, shots):
        arrived.append(lax.ppermute(pieces[index], "shot", [(i, i ^ index) for i in range(shots)]))
    (result,) = call(functools.partial(combine, shots), (sds(n, 128 // shots, 64),), [], *arrived)
    return result


def solution(mesh):
    placed = (
        P("shot", "pair", None, "space", None, None),
        P("space", None, None),
        P("shot", None, "space", None),
    )
    return jax.shard_map(on_device, mesh=mesh, in_specs=placed, out_specs=P("space", "shot", "pair"), check_vma=False)
```
